32 devices in a mesh: section: 2 (over core), ctx: 4 (over z), tp: 4 (over y, x).
Axes of the slice: x: 2, y: 2, z: 4, core: 2. Of those that a mesh axis runs over, the one named last changes fastest.
Arguments:
- activations: bfloat16 [2, 512, 2048], P(None, 'ctx'), may hold values from -6 to 6
- positions: int32 [2, 512], P(None, 'ctx'), may hold values from 0 to 1023, as said below
- cotangent: bfloat16 [2, 512, 2048], P(None, 'ctx'), may hold values from -6 to 6
- attn_gain: bfloat16 [2, 2048], P('section', 'ctx'), may hold values from 0.099609375 to 1.8984375
- w_query: bfloat16 [2, 2048, 2048], P('section', 'ctx', 'tp'), may hold values from -0.125 to 0.125
- w_keyval: bfloat16 [2, 2048, 4, 128], P('section', 'ctx', 'tp'), may hold values from -0.125 to 0.125
- w_out: bfloat16 [2, 2048, 2048], P('section', 'tp', 'ctx'), may hold values from -0.5 to 0.5
- ffn_gain: bfloat16 [2, 2048], P('section', 'ctx'), may hold values from 0.099609375 to 1.8984375
- w_gate: bfloat16 [2, 2048, 5632], P('section', 'ctx', 'tp'), may hold values from -0.125 to 0.125
- w_up: bfloat16 [2, 2048, 5632], P('section', 'ctx', 'tp'), may hold values from -0.125 to 0.125
- w_down: bfloat16 [2, 5632, 2048], P('section', 'tp', 'ctx'), may hold values from -0.078125 to 0.078125
Outputs:
- section_out: bfloat16 [2, 2, 512, 2048], P('section', None, 'ctx')
- input_grad: bfloat16 [2, 2, 512, 2048], P('section', None, 'ctx')
- grad_attn_gain: float32 [2, 2048], P('section', 'ctx')
- grad_query: float32 [2, 2048, 2048], P('section', 'ctx', 'tp')
- grad_keyval: float32 [2, 2048, 4, 128], P('section', 'ctx', 'tp')
- grad_out: float32 [2, 2048, 2048], P('section', 'tp', 'ctx')
- grad_ffn_gain: float32 [2, 2048], P('section', 'ctx')
- grad_gate: float32 [2, 2048, 5632], P('section', 'ctx', 'tp')
- grad_up: float32 [2, 2048, 5632], P('section', 'ctx', 'tp')
- grad_down: float32 [2, 5632, 2048], P('section', 'tp', 'ctx')
The draws below stay inside these ranges and needn't reach their ends.
Inputs may be any that keep to these rules, and one draw needn't show every extreme that they name: In each sequence the positions rise by 1, 2 or 3 from token to token; the first is 0 and the last 1023.
All inputs are finite; a program needn't handle non-finite values.
Results may differ from the reference program's by a relative error of at most 0.04.
Values may be sent and summed in bfloat16 or wider, within the bound.
No kernel may reach another device: no remote copies, remote signals or barrier semaphores. Data moves between devices by JAX's collectives and lax.ppermute only.
A program may use at most 192 MiB of HBM per device.

```python
import jax
import jax.numpy as jnp
from jax import lax

MODEL_WIDTH = 2048
QUERY_HEADS = 32
KEY_VALUE_HEADS = 4
HEAD_WIDTH = 64
FF = 5632
MB = 2
LAYER_COUNT = 2
SEQUENCE_LENGTH = 512


def draw_positions(key, part):
    offsets_bit = jax.random.randint(key, (MB, SEQUENCE_LENGTH), 0, 2)
    token_index = jnp.arange(SEQUENCE_LENGTH, dtype=jnp.int32)
    offsets_bit = jnp.where(token_index[None, :] == 0, 0, offsets_bit)
    offsets_bit = jnp.where(token_index[None, :] == SEQUENCE_LENGTH - 1, 1, offsets_bit)
    return (2 * token_index[None, :] + offsets_bit).astype(jnp.int32)


def block_scale(key, dims, pieces, low, largest):
    def one(axis_at, blocks):
        draws = jax.random.uniform(jax.random.fold_in(jax.random.fold_in(key, 6), axis_at), (blocks,), jnp.float32, low / len(pieces), largest / len(pieces))
        return jnp.repeat(jnp.exp(draws), dims[axis_at] // blocks).reshape((-1,) + (1,) * (len(dims) - axis_at - 1))

    gain = one(*pieces[0])
    for cut in pieces[1:]:
        gain = gain * one(*cut)
    return gain


def gaussian(stream_key, dims, width, bound, shards=(), held_as=jnp.bfloat16):
    entries = jax.random.normal(stream_key, dims, jnp.float32) * width
    if len(shards) > 0:
        entries = block_scale(stream_key, dims, shards, -0.22, 0.18) * entries
    return jnp.clip(entries, min=-bound, max=bound).astype(held_as)


def setup_inputs(seed: int = 0) -> dict:
    keys = jax.random.split(jax.random.key(seed), 12)
    return {
        "activations": gaussian(keys[0], (MB, SEQUENCE_LENGTH, MODEL_WIDTH), 1.0, 6.0, ((1, 4),)),
        "positions": draw_positions(jax.random.fold_in(keys[11], 71), 0),
        "cotangent": gaussian(keys[2], (MB, SEQUENCE_LENGTH, MODEL_WIDTH), 1.0, 6.0, ((1, 4),)),
        "attn_gain": jnp.clip(1.0 + 0.18 * jax.random.normal(keys[3], (LAYER_COUNT, MODEL_WIDTH), jnp.float32), 0.099609375, 1.8984375).astype(jnp.bfloat16),
        "w_query": gaussian(keys[4], (LAYER_COUNT, MODEL_WIDTH, QUERY_HEADS * HEAD_WIDTH), MODEL_WIDTH ** -0.5, 0.125, ((0, 2), (1, 4), (2, 4))),
        "w_keyval": gaussian(keys[5], (LAYER_COUNT, MODEL_WIDTH, KEY_VALUE_HEADS, 2 * HEAD_WIDTH), MODEL_WIDTH ** -0.5, 0.125, ((0, 2), (1, 4), (2, 4))),
        "w_out": gaussian(keys[6], (LAYER_COUNT, QUERY_HEADS * HEAD_WIDTH, MODEL_WIDTH), (max(1, QUERY_HEADS * HEAD_WIDTH * 32 // SEQUENCE_LENGTH)) ** -0.5, 0.5, ((0, 2), (1, 4), (2, 4))),
        "ffn_gain": jnp.clip(1.0 + 0.18 * jax.random.normal(keys[7], (LAYER_COUNT, MODEL_WIDTH), jnp.float32), 0.099609375, 1.8984375).astype(jnp.bfloat16),
        "w_gate": gaussian(keys[8], (LAYER_COUNT, MODEL_WIDTH, FF), MODEL_WIDTH ** -0.5, 0.125, ((0, 2), (1, 4), (2, 4))),
        "w_up": gaussian(keys[9], (LAYER_COUNT, MODEL_WIDTH, FF), MODEL_WIDTH ** -0.5, 0.125, ((0, 2), (1, 4), (2, 4))),
        "w_down": gaussian(keys[10], (LAYER_COUNT, FF, MODEL_WIDTH), FF ** -0.5, 0.078125, ((0, 2), (1, 4), (2, 4))),
    }


EPS = 1e-05
ROPE_BASE = 10000.0
NEG = -1e+30

def rope_tables(token_pos):
    half_dim = HEAD_WIDTH // 2
    frequency = ROPE_BASE ** (-(2.0 * jnp.arange(half_dim).astype(jnp.float32)) / HEAD_WIDTH)
    angles = token_pos.astype(jnp.float32)[:, None] * frequency[None, :]
    return (jnp.cos(angles)[:, None, :], jnp.sin(angles)[:, None, :])

def rotate(tensor, cosine, sine_part):
    front_half = tensor[..., :HEAD_WIDTH // 2]
    back_half = tensor[..., HEAD_WIDTH // 2:]
    return jnp.concatenate([front_half * cosine - back_half * sine_part, back_half * cosine + front_half * sine_part], axis=-1)

def norm_forward(inputs_f, gain_row):
    mean_sq = lax.optimization_barrier(jnp.mean(inputs_f * inputs_f, axis=-1, keepdims=True))
    inv_rms = lax.rsqrt(mean_sq + EPS)
    normed = inputs_f * inv_rms
    return (normed, inv_rms, (normed * gain_row.astype(jnp.float32)).astype(jnp.bfloat16))

def norm_backward(upstream_f, normed, inv_rms, gain_row):
    scaled = upstream_f * gain_row.astype(jnp.float32)
    gain_grad = lax.optimization_barrier(jnp.sum(upstream_f * normed, axis=0))
    inner = lax.optimization_barrier(jnp.mean(scaled * normed, axis=-1, keepdims=True))
    return (gain_grad, inv_rms * (scaled - normed * inner))

def block_layout():
    rows_per_block = min(512, SEQUENCE_LENGTH)
    blocks_count = SEQUENCE_LENGTH // rows_per_block
    block_starts = (jnp.arange(blocks_count) * rows_per_block).astype(jnp.int32)
    return (rows_per_block, blocks_count, block_starts)

def attend_forward(query_rows, key_rows, value_rows):
    rows_per_block, blocks_count, block_starts = block_layout()
    query_group_width = QUERY_HEADS // KEY_VALUE_HEADS
    query_per_block = query_rows.reshape(blocks_count, rows_per_block, KEY_VALUE_HEADS, query_group_width, HEAD_WIDTH)
    key_index = jnp.arange(SEQUENCE_LENGTH).astype(jnp.int32)

    def block_pass(packed):
        query_block, offset = packed
        scores = jnp.einsum('qhgd,khd->hgqk', query_block.astype(jnp.float32), key_rows.astype(jnp.float32)) * 0.125
        query_index = offset + jnp.arange(rows_per_block).astype(jnp.int32)
        causal = key_index[None, :] <= query_index[:, None]
        scores = jnp.where(causal, scores, NEG)
        row_max = lax.optimization_barrier(jnp.max(scores, axis=-1, keepdims=True))
        weights_now = jnp.where(causal, jnp.exp(scores - row_max), 0.0)
        row_total = lax.optimization_barrier(jnp.sum(weights_now, axis=-1, keepdims=True))
        logarithm_total = row_max + jnp.log(row_total)
        probs = (weights_now / row_total).astype(jnp.bfloat16)
        attention_output = jnp.einsum('hgqk,khd->qhgd', probs.astype(jnp.float32), value_rows.astype(jnp.float32))
        return (attention_output.astype(jnp.bfloat16), logarithm_total[..., 0])
    block_outputs, block_logsumexp = lax.map(block_pass, (query_per_block, block_starts))
    attention_output = block_outputs.reshape(SEQUENCE_LENGTH, KEY_VALUE_HEADS, query_group_width, HEAD_WIDTH)
    logarithm_total = jnp.transpose(block_logsumexp, (1, 2, 0, 3)).reshape(KEY_VALUE_HEADS, query_group_width, SEQUENCE_LENGTH)
    return (attention_output, logarithm_total)

def attend_backward(query_rows, key_rows, value_rows, attention_output, logarithm_total, attention_output_gradient):
    rows_per_block, blocks_count, block_starts = block_layout()
    query_group_width = QUERY_HEADS // KEY_VALUE_HEADS
    query_per_block = query_rows.reshape(blocks_count, rows_per_block, KEY_VALUE_HEADS, query_group_width, HEAD_WIDTH)
    output_per_block = attention_output.reshape(blocks_count, rows_per_block, KEY_VALUE_HEADS, query_group_width, HEAD_WIDTH)
    gradient_per_block = attention_output_gradient.reshape(blocks_count, rows_per_block, KEY_VALUE_HEADS, query_group_width, HEAD_WIDTH)
    logsumexp_per_block = jnp.transpose(logarithm_total.reshape(KEY_VALUE_HEADS, query_group_width, blocks_count, rows_per_block), (2, 0, 1, 3))
    key_index = jnp.arange(SEQUENCE_LENGTH).astype(jnp.int32)
    keys_f = key_rows.astype(jnp.float32)
    values_f = value_rows.astype(jnp.float32)

    def block_pass(keyvalue_gradient, packed):
        query_block, out_block, grad_block, lse_block, offset = packed
        scores = jnp.einsum('qhgd,khd->hgqk', query_block.astype(jnp.float32), keys_f) * 0.125
        query_index = offset + jnp.arange(rows_per_block).astype(jnp.int32)
        causal = key_index[None, :] <= query_index[:, None]
        scores = jnp.where(causal, scores, NEG)
        probs = jnp.where(causal, jnp.exp(scores - lse_block[..., None]), 0.0)
        probs_bf = probs.astype(jnp.bfloat16)
        delta_sum = jnp.transpose(lax.optimization_barrier(jnp.sum(grad_block.astype(jnp.float32) * out_block.astype(jnp.float32), axis=-1)), (1, 2, 0))
        d_prob = jnp.einsum('qhgd,khd->hgqk', grad_block.astype(jnp.float32), values_f)
        d_score = (probs * (d_prob - delta_sum[..., None]) * 0.125).astype(jnp.bfloat16)
        query_gradient = jnp.einsum('hgqk,khd->qhgd', d_score.astype(jnp.float32), keys_f)
        key_gradient = jnp.einsum('hgqk,qhgd->khd', d_score.astype(jnp.float32), query_block.astype(jnp.float32))
        d_value = jnp.einsum('hgqk,qhgd->khd', probs_bf.astype(jnp.float32), grad_block.astype(jnp.float32))
        return (keyvalue_gradient + jnp.concatenate([key_gradient, d_value], axis=-1), query_gradient)
    initial_state = jnp.zeros((SEQUENCE_LENGTH, KEY_VALUE_HEADS, 2 * HEAD_WIDTH), jnp.float32)
    keyvalue_gradient, query_gradient = lax.scan(block_pass, initial_state, (query_per_block, output_per_block, gradient_per_block, logsumexp_per_block, block_starts))
    return (query_gradient.reshape(SEQUENCE_LENGTH, QUERY_HEADS, HEAD_WIDTH), keyvalue_gradient)

def layer_forward(layer_in, token_pos, weights):
    gain_attn, query_weight, key_value_weight, weight_out, gain_ffn, weight_gate, weight_up, weight_down = weights
    inputs_f = layer_in.astype(jnp.float32)
    normed1, inv_rms1, first_normed_bfloat = norm_forward(inputs_f, gain_attn)
    cosine, sine_part = rope_tables(token_pos)
    query_proj = jnp.dot(first_normed_bfloat, query_weight, preferred_element_type=jnp.float32).reshape(SEQUENCE_LENGTH, QUERY_HEADS, HEAD_WIDTH)
    key_value_projection = jnp.dot(first_normed_bfloat, key_value_weight.reshape(MODEL_WIDTH, KEY_VALUE_HEADS * 2 * HEAD_WIDTH), preferred_element_type=jnp.float32).reshape(SEQUENCE_LENGTH, KEY_VALUE_HEADS, 2 * HEAD_WIDTH)
    query_rows = rotate(query_proj, cosine, sine_part).astype(jnp.bfloat16)
    key_rows = rotate(key_value_projection[..., :HEAD_WIDTH], cosine, sine_part).astype(jnp.bfloat16)
    value_rows = key_value_projection[..., HEAD_WIDTH:].astype(jnp.bfloat16)
    query_rows = query_rows.reshape(SEQUENCE_LENGTH, KEY_VALUE_HEADS, QUERY_HEADS // KEY_VALUE_HEADS, HEAD_WIDTH)
    attention_output, logarithm_total = attend_forward(query_rows, key_rows, value_rows)
    hidden1 = inputs_f + jnp.dot(attention_output.reshape(SEQUENCE_LENGTH, QUERY_HEADS * HEAD_WIDTH), weight_out, preferred_element_type=jnp.float32)
    normed2, inv_rms2, normed_bf2 = norm_forward(hidden1, gain_ffn)
    gate_pre = jnp.dot(normed_bf2, weight_gate, preferred_element_type=jnp.float32)
    up_value = jnp.dot(normed_bf2, weight_up, preferred_element_type=jnp.float32)
    hidden = (jax.nn.silu(gate_pre) * up_value).astype(jnp.bfloat16)
    result = (hidden1 + jnp.dot(hidden, weight_down, preferred_element_type=jnp.float32)).astype(jnp.bfloat16)
    saved = (normed1, inv_rms1, first_normed_bfloat, query_rows, key_rows, value_rows, attention_output, logarithm_total, normed2, inv_rms2, normed_bf2, gate_pre, up_value, hidden, cosine, sine_part)
    return (result, saved)

def layer_backward(upstream, weights, saved):
    gain_attn, query_weight, key_value_weight, weight_out, gain_ffn, weight_gate, weight_up, weight_down = weights
    normed1, inv_rms1, first_normed_bfloat, query_rows, key_rows, value_rows, attention_output, logarithm_total, normed2, inv_rms2, normed_bf2, gate_pre, up_value, hidden, cosine, sine_part = saved
    upstream_f = upstream.astype(jnp.float32)
    d_hidden = jnp.dot(upstream, weight_down.T, preferred_element_type=jnp.float32)
    grad_down = jnp.dot(hidden.T, upstream, preferred_element_type=jnp.float32)
    sigma = jax.nn.sigmoid(gate_pre)
    d_gate = (d_hidden * up_value * sigma * (1.0 + gate_pre * (1.0 - sigma))).astype(jnp.bfloat16)
    d_up = (d_hidden * gate_pre * sigma).astype(jnp.bfloat16)
    grad_gate = jnp.dot(normed_bf2.T, d_gate, preferred_element_type=jnp.float32)
    grad_up = jnp.dot(normed_bf2.T, d_up, preferred_element_type=jnp.float32)
    d_norm2 = jnp.dot(d_gate, weight_gate.T, preferred_element_type=jnp.float32) + jnp.dot(d_up, weight_up.T, preferred_element_type=jnp.float32)
    grad_gain2, d_resid = norm_backward(d_norm2, normed2, inv_rms2, gain_ffn)
    d_hidden1 = upstream_f + d_resid
    d_hidden_bf = d_hidden1.astype(jnp.bfloat16)
    flat_attended = attention_output.reshape(SEQUENCE_LENGTH, QUERY_HEADS * HEAD_WIDTH)
    grad_out = jnp.dot(flat_attended.T, d_hidden_bf, preferred_element_type=jnp.float32)
    attention_output_gradient = jnp.dot(d_hidden_bf, weight_out.T, preferred_element_type=jnp.float32).astype(jnp.bfloat16)
    attention_output_gradient = attention_output_gradient.reshape(SEQUENCE_LENGTH, KEY_VALUE_HEADS, QUERY_HEADS // KEY_VALUE_HEADS, HEAD_WIDTH)
    d_query_raw, keyvalue_gradient = attend_backward(query_rows, key_rows, value_rows, attention_output, logarithm_total, attention_output_gradient)
    query_gradient = rotate(d_query_raw, cosine, -sine_part).astype(jnp.bfloat16).reshape(SEQUENCE_LENGTH, QUERY_HEADS * HEAD_WIDTH)
    key_gradient = rotate(keyvalue_gradient[..., :HEAD_WIDTH], cosine, -sine_part)
    key_value_gradient = jnp.concatenate([key_gradient, keyvalue_gradient[..., HEAD_WIDTH:]], axis=-1).astype(jnp.bfloat16).reshape(SEQUENCE_LENGTH, KEY_VALUE_HEADS * 2 * HEAD_WIDTH)
    grad_query = jnp.dot(first_normed_bfloat.T, query_gradient, preferred_element_type=jnp.float32)
    key_value_grads = jnp.dot(first_normed_bfloat.T, key_value_gradient, preferred_element_type=jnp.float32).reshape(MODEL_WIDTH, KEY_VALUE_HEADS, 2 * HEAD_WIDTH)
    first_norm_gradient = jnp.dot(query_gradient, query_weight.T, preferred_element_type=jnp.float32) + jnp.dot(key_value_gradient, key_value_weight.reshape(MODEL_WIDTH, KEY_VALUE_HEADS * 2 * HEAD_WIDTH).T, preferred_element_type=jnp.float32)
    grad_gain1, d_front = norm_backward(first_norm_gradient, normed1, inv_rms1, gain_attn)
    d_input = (d_hidden1 + d_front).astype(jnp.bfloat16)
    return (d_input, (grad_gain1, grad_query, key_value_grads, grad_out, grad_gain2, grad_gate, grad_up, grad_down))

def reference(activations, positions, cotangent, attn_gain, w_query, w_keyval, w_out, ffn_gain, w_gate, w_up, w_down):
    layer_params = [(attn_gain[layer_idx], w_query[layer_idx], w_keyval[layer_idx], w_out[layer_idx], ffn_gain[layer_idx], w_gate[layer_idx], w_up[layer_idx], w_down[layer_idx]) for layer_idx in range(LAYER_COUNT)]
    grad_sums = [[jnp.zeros(piece_now.shape, jnp.float32) for piece_now in layer_params[layer_idx]] for layer_idx in range(LAYER_COUNT)]
    outs_front, outs_back, grads_front, grads_back = ([], [], [], [])
    for micro_idx in range(MB):
        first_out, first_saved = layer_forward(activations[micro_idx], positions[micro_idx], layer_params[0])
        second_out, second_saved = layer_forward(first_out, positions[micro_idx], layer_params[1])
        second_grad, second_terms = layer_backward(cotangent[micro_idx], layer_params[1], second_saved)
        first_grad, first_terms = layer_backward(second_grad, layer_params[0], first_saved)
        outs_front.append(first_out)
        outs_back.append(second_out)
        grads_front.append(first_grad)
        grads_back.append(second_grad)
        grad_sums[0] = [total_now + term_now for total_now, term_now in zip(grad_sums[0], first_terms)]
        grad_sums[1] = [total_now + term_now for total_now, term_now in zip(grad_sums[1], second_terms)]
    section_out = jnp.stack([jnp.stack(outs_front), jnp.stack(outs_back)])
    input_grad = jnp.stack([jnp.stack(grads_front), jnp.stack(grads_back)])
    stacked = [jnp.stack([grad_sums[0][index_now], grad_sums[1][index_now]]) for index_now in range(8)]
    return (section_out, input_grad, stacked[0], stacked[1], stacked[2], stacked[3], stacked[4], stacked[5], stacked[6], stacked[7])
```

```python
import jax
import jax.numpy as jnp
from jax import lax
from jax.sharding import PartitionSpec as P

HEAD_WIDTH = 64


EPS = 1e-05
ROPE_BASE = 10000.0
NEG = -1e30


def passed_along(value, axis, steps):
    count = lax.axis_size(axis)
    initial, last = (max(0, -steps), min(count, count - steps))
    return lax.ppermute(value, axis, [(source, source + steps) for source in range(initial, last)])


def rope_tables(token_pos):
    half_dim = HEAD_WIDTH // 2
    frequency = ROPE_BASE ** (-(2.0 * jnp.arange(half_dim).astype(jnp.float32)) / HEAD_WIDTH)
    angles = token_pos.astype(jnp.float32)[:, None] * frequency[None, :]
    return (jnp.cos(angles)[:, None, :], jnp.sin(angles)[:, None, :])


def rotate(tensor, cosine, sine_part):
    front_half = tensor[..., : HEAD_WIDTH // 2]
    back_half = tensor[..., HEAD_WIDTH // 2 :]
    return jnp.concatenate(
        [front_half * cosine - back_half * sine_part, back_half * cosine + front_half * sine_part],
        axis=-1,
    )


def norm_forward(inputs_f, gain_row):
    mean_sq = jnp.mean(inputs_f * inputs_f, axis=-1, keepdims=True)
    inv_rms = lax.rsqrt(mean_sq + EPS)
    normed = inputs_f * inv_rms
    return (normed, inv_rms, (normed * gain_row.astype(jnp.float32)).astype(jnp.bfloat16))


def norm_backward(upstream_f, normed, inv_rms, gain_row):
    scaled = upstream_f * gain_row.astype(jnp.float32)
    gain_grad = jnp.sum(upstream_f * normed, axis=0)
    inner = jnp.mean(scaled * normed, axis=-1, keepdims=True)
    return (gain_grad, inv_rms * (scaled - normed * inner))


def head_sum(partial_now):
    return lax.psum(partial_now.astype(jnp.bfloat16), "tp").astype(jnp.float32)


def forward_layer(layer_in, token_pos, weights):
    (
        gain_attn,
        query_weight,
        key_value_weight,
        weight_out,
        gain_ffn,
        weight_gate,
        weight_up,
        weight_down,
    ) = weights
    token_rows = layer_in.shape[0]
    kv_local = key_value_weight.shape[1]
    heads_local = query_weight.shape[1] // HEAD_WIDTH
    query_group_width = heads_local // kv_local
    first_row = lax.axis_index("ctx") * token_rows
    inputs_f = layer_in.astype(jnp.float32)
    normed1, inv_rms1, first_normed_bfloat = norm_forward(inputs_f, gain_attn)
    cosine, sine_part = rope_tables(token_pos)
    query_proj = jnp.dot(
        first_normed_bfloat, query_weight, preferred_element_type=jnp.float32
    ).reshape(token_rows, heads_local, HEAD_WIDTH)
    key_value_projection = jnp.dot(
        first_normed_bfloat,
        key_value_weight.reshape(key_value_weight.shape[0], -1),
        preferred_element_type=jnp.float32,
    ).reshape(token_rows, kv_local, 2 * HEAD_WIDTH)
    query_rows = (
        rotate(query_proj, cosine, sine_part)
        .astype(jnp.bfloat16)
        .reshape(token_rows, kv_local, query_group_width, HEAD_WIDTH)
    )
    key_rows = rotate(key_value_projection[..., :HEAD_WIDTH], cosine, sine_part).astype(
        jnp.bfloat16
    )
    kv_block = jnp.concatenate(
        [key_rows, key_value_projection[..., HEAD_WIDTH:].astype(jnp.bfloat16)], axis=-1
    )
    query_index = first_row + jnp.arange(token_rows, dtype=jnp.int32)
    kv_piece = lax.all_gather(kv_block, "ctx", axis=0, tiled=True)
    row_max = jnp.full((kv_local, query_group_width, token_rows), NEG, jnp.float32)
    key_part = kv_piece[..., :HEAD_WIDTH]
    value_part = kv_piece[..., HEAD_WIDTH:]
    scores = (
        jnp.einsum("qhgd,khd->hgqk", query_rows, key_part, preferred_element_type=jnp.float32)
        * 0.125
    )
    key_index = jnp.arange(kv_piece.shape[0], dtype=jnp.int32)
    causal = key_index[None, :] <= query_index[:, None]
    scores = jnp.where(causal, scores, NEG)
    new_max = jnp.maximum(row_max, jnp.max(scores, axis=-1))
    weights_now = jnp.where(causal, jnp.exp(scores - new_max[..., None]), 0.0)
    row_total = jnp.sum(weights_now, axis=-1)
    weighted = jnp.einsum(
        "hgqk,khd->hgqd",
        weights_now.astype(jnp.bfloat16),
        value_part,
        preferred_element_type=jnp.float32,
    )
    row_max, row_total, weighted = (new_max, row_total, weighted)
    logarithm_total = row_max + jnp.log(row_total)
    attention_output = jnp.transpose(weighted / row_total[..., None], (2, 0, 1, 3)).astype(
        jnp.bfloat16
    )
    hidden1 = inputs_f + head_sum(
        jnp.dot(
            attention_output.reshape(token_rows, -1), weight_out, preferred_element_type=jnp.float32
        )
    )
    normed2, inv_rms2, normed_bf2 = norm_forward(hidden1, gain_ffn)
    gate_pre = jnp.dot(normed_bf2, weight_gate, preferred_element_type=jnp.float32)
    up_value = jnp.dot(normed_bf2, weight_up, preferred_element_type=jnp.float32)
    hidden = (jax.nn.silu(gate_pre) * up_value).astype(jnp.bfloat16)
    result = (
        hidden1 + head_sum(jnp.dot(hidden, weight_down, preferred_element_type=jnp.float32))
    ).astype(jnp.bfloat16)
    saved = (
        normed1,
        inv_rms1,
        first_normed_bfloat,
        query_rows,
        kv_block,
        attention_output,
        logarithm_total,
        normed2,
        inv_rms2,
        normed_bf2,
        gate_pre,
        up_value,
        hidden,
        cosine,
        sine_part,
    )
    return (result, saved)


def backward_layer(upstream, weights, saved):
    (
        gain_attn,
        query_weight,
        key_value_weight,
        weight_out,
        gain_ffn,
        weight_gate,
        weight_up,
        weight_down,
    ) = weights
    (
        normed1,
        inv_rms1,
        first_normed_bfloat,
        query_rows,
        kv_block,
        attention_output,
        logarithm_total,
        normed2,
        inv_rms2,
        normed_bf2,
        gate_pre,
        up_value,
        hidden,
        cosine,
        sine_part,
    ) = saved
    token_rows = upstream.shape[0]
    kv_local = kv_block.shape[1]
    query_group_width = query_rows.shape[2]
    first_row = lax.axis_index("ctx") * token_rows
    upstream_f = upstream.astype(jnp.float32)
    d_hidden = jnp.dot(upstream, weight_down.T, preferred_element_type=jnp.float32)
    grad_down = jnp.dot(hidden.T, upstream, preferred_element_type=jnp.float32)
    sigma = jax.nn.sigmoid(gate_pre)
    d_gate = (d_hidden * up_value * sigma * (1.0 + gate_pre * (1.0 - sigma))).astype(jnp.bfloat16)
    d_up = (d_hidden * gate_pre * sigma).astype(jnp.bfloat16)
    grad_gate = jnp.dot(normed_bf2.T, d_gate, preferred_element_type=jnp.float32)
    grad_up = jnp.dot(normed_bf2.T, d_up, preferred_element_type=jnp.float32)
    d_norm2 = head_sum(
        jnp.dot(d_gate, weight_gate.T, preferred_element_type=jnp.float32)
        + jnp.dot(d_up, weight_up.T, preferred_element_type=jnp.float32)
    )
    grad_gain2, d_resid = norm_backward(d_norm2, normed2, inv_rms2, gain_ffn)
    d_hidden1 = upstream_f + d_resid
    d_hidden_bf = d_hidden1.astype(jnp.bfloat16)
    grad_out = jnp.dot(
        attention_output.reshape(token_rows, -1).T, d_hidden_bf, preferred_element_type=jnp.float32
    )
    attention_output_gradient = jnp.dot(
        d_hidden_bf, weight_out.T, preferred_element_type=jnp.float32
    ).astype(jnp.bfloat16)
    attention_output_gradient = attention_output_gradient.reshape(
        token_rows, kv_local, query_group_width, HEAD_WIDTH
    )
    kv_whole = lax.all_gather(kv_block, "ctx", axis=0, tiled=True)
    total_rows = kv_whole.shape[0]
    key_rows_block = min(512, total_rows)
    block_count = total_rows // key_rows_block
    kv_blocks = kv_whole.reshape(block_count, key_rows_block, kv_local, 2 * HEAD_WIDTH)
    block_starts = jnp.arange(block_count, dtype=jnp.int32) * key_rows_block
    query_index = first_row + jnp.arange(token_rows, dtype=jnp.int32)
    delta_sum = jnp.transpose(
        jnp.sum(
            attention_output_gradient.astype(jnp.float32) * attention_output.astype(jnp.float32),
            axis=-1,
        ),
        (1, 2, 0),
    )

    def key_block(d_query_acc, packed):
        kv_piece, offset = packed
        key_part = kv_piece[..., :HEAD_WIDTH]
        value_part = kv_piece[..., HEAD_WIDTH:]
        key_index = offset + jnp.arange(key_rows_block, dtype=jnp.int32)
        causal = key_index[None, :] <= query_index[:, None]
        scores = (
            jnp.einsum("qhgd,khd->hgqk", query_rows, key_part, preferred_element_type=jnp.float32)
            * 0.125
        )
        scores = jnp.where(causal, scores, NEG)
        probs = jnp.where(causal, jnp.exp(scores - logarithm_total[..., None]), 0.0)
        probs_bf = probs.astype(jnp.bfloat16)
        d_prob = jnp.einsum(
            "qhgd,khd->hgqk",
            attention_output_gradient,
            value_part,
            preferred_element_type=jnp.float32,
        )
        d_score = (probs * (d_prob - delta_sum[..., None]) * 0.125).astype(jnp.bfloat16)
        d_query_acc = d_query_acc + jnp.einsum(
            "hgqk,khd->qhgd", d_score, key_part, preferred_element_type=jnp.float32
        )
        key_gradient = jnp.einsum(
            "hgqk,qhgd->khd", d_score, query_rows, preferred_element_type=jnp.float32
        )
        d_value = jnp.einsum(
            "hgqk,qhgd->khd",
            probs_bf,
            attention_output_gradient,
            preferred_element_type=jnp.float32,
        )
        return (d_query_acc, jnp.concatenate([key_gradient, d_value], axis=-1))

    query_start = jnp.zeros((token_rows, kv_local, query_group_width, HEAD_WIDTH), jnp.float32)
    d_query_raw, kv_terms = lax.scan(key_block, query_start, (kv_blocks, block_starts))
    kv_terms = kv_terms.reshape(total_rows, kv_local, 2 * HEAD_WIDTH)
    keyvalue_gradient = lax.psum_scatter(
        kv_terms.astype(jnp.bfloat16), "ctx", scatter_dimension=0, tiled=True
    ).astype(jnp.float32)
    query_gradient = (
        rotate(d_query_raw.reshape(token_rows, -1, HEAD_WIDTH), cosine, -sine_part)
        .astype(jnp.bfloat16)
        .reshape(token_rows, -1)
    )
    d_key_rot = rotate(keyvalue_gradient[..., :HEAD_WIDTH], cosine, -sine_part)
    key_value_gradient = (
        jnp.concatenate([d_key_rot, keyvalue_gradient[..., HEAD_WIDTH:]], axis=-1)
        .astype(jnp.bfloat16)
        .reshape(token_rows, -1)
    )
    grad_query = jnp.dot(first_normed_bfloat.T, query_gradient, preferred_element_type=jnp.float32)
    key_value_grads = jnp.dot(
        first_normed_bfloat.T, key_value_gradient, preferred_element_type=jnp.float32
    ).reshape(key_value_weight.shape)
    first_norm_gradient = head_sum(
        jnp.dot(query_gradient, query_weight.T, preferred_element_type=jnp.float32)
        + jnp.dot(
            key_value_gradient,
            key_value_weight.reshape(key_value_weight.shape[0], -1).T,
            preferred_element_type=jnp.float32,
        )
    )
    grad_gain1, d_front = norm_backward(first_norm_gradient, normed1, inv_rms1, gain_attn)
    d_input = (d_hidden1 + d_front).astype(jnp.bfloat16)
    return (
        d_input,
        (
            grad_gain1,
            grad_query,
            key_value_grads,
            grad_out,
            grad_gain2,
            grad_gate,
            grad_up,
            grad_down,
        ),
    )


def on_device(
    activations,
    positions,
    cotangent,
    attn_gain,
    w_query,
    w_keyval,
    w_out,
    ffn_gain,
    w_gate,
    w_up,
    w_down,
):
    front_section = lax.axis_index("section") == 0
    micro_count = activations.shape[0]
    local_parts = (
        attn_gain[0],
        w_query[0],
        w_keyval[0],
        w_out[0],
        ffn_gain[0],
        w_gate[0],
        w_up[0],
        w_down[0],
    )
    forward_weights = (
        lax.all_gather(local_parts[0], "ctx", axis=0, tiled=True),
        lax.all_gather(local_parts[1], "ctx", axis=0, tiled=True),
        lax.all_gather(local_parts[2], "ctx", axis=0, tiled=True),
        lax.all_gather(local_parts[3], "ctx", axis=1, tiled=True),
        lax.all_gather(local_parts[4], "ctx", axis=0, tiled=True),
        lax.all_gather(local_parts[5], "ctx", axis=0, tiled=True),
        lax.all_gather(local_parts[6], "ctx", axis=0, tiled=True),
        lax.all_gather(local_parts[7], "ctx", axis=1, tiled=True),
    )
    arrived = jnp.zeros_like(activations[0])
    results = []
    kept = []
    for moment in range(micro_count + 1):
        later = min(moment, micro_count - 1)
        earlier = max(moment - 1, 0)
        layer_in = jnp.where(front_section, activations[later], arrived)
        layer_pos = jnp.where(front_section, positions[later], positions[earlier])
        produced, saved = forward_layer(layer_in, layer_pos, forward_weights)
        results.append(produced)
        kept.append(saved)
        arrived = passed_along(produced, "section", 1)
    backward_weights = (
        lax.all_gather(local_parts[0], "ctx", axis=0, tiled=True),
        lax.all_gather(local_parts[1], "ctx", axis=0, tiled=True),
        lax.all_gather(local_parts[2], "ctx", axis=0, tiled=True),
        lax.all_gather(local_parts[3], "ctx", axis=1, tiled=True),
        lax.all_gather(local_parts[4], "ctx", axis=0, tiled=True),
        lax.all_gather(local_parts[5], "ctx", axis=0, tiled=True),
        lax.all_gather(local_parts[6], "ctx", axis=0, tiled=True),
        lax.all_gather(local_parts[7], "ctx", axis=1, tiled=True),
    )
    grad_sums = tuple((jnp.zeros(shard_now.shape, jnp.float32) for shard_now in backward_weights))
    reduced = tuple((jnp.zeros(shard_now.shape, jnp.float32) for shard_now in local_parts))
    returned = jnp.zeros_like(cotangent[0])
    sent = []
    for moment in range(micro_count + 1):
        later = min(moment, micro_count - 1)
        earlier = max(moment - 1, 0)
        upstream = jnp.where(front_section, returned, cotangent[later])
        saved = jax.tree.map(
            lambda front_val, back_val: jnp.where(front_section, front_val, back_val),
            kept[earlier],
            kept[later + 1],
        )
        live = jnp.where(front_section, moment >= 1, moment < micro_count)
        d_input, layer_grads = backward_layer(upstream, backward_weights, saved)
        grad_sums = tuple(
            (
                jnp.where(live, total_now + grad_now, total_now)
                for total_now, grad_now in zip(grad_sums, layer_grads)
            )
        )
        sent.append(d_input)
        returned = passed_along(d_input, "section", -1)
    section_out = jnp.stack(
        [
            jnp.where(front_section, results[micro_idx], results[micro_idx + 1])
            for micro_idx in range(micro_count)
        ]
    )
    input_grad = jnp.stack(
        [
            jnp.where(front_section, sent[micro_idx + 1], sent[micro_idx])
            for micro_idx in range(micro_count)
        ]
    )
    reduced = (
        lax.psum_scatter(
            grad_sums[0].astype(jnp.bfloat16), "ctx", scatter_dimension=0, tiled=True
        ).astype(jnp.float32),
        lax.psum_scatter(
            grad_sums[1].astype(jnp.bfloat16), "ctx", scatter_dimension=0, tiled=True
        ).astype(jnp.float32),
        lax.psum_scatter(
            grad_sums[2].astype(jnp.bfloat16), "ctx", scatter_dimension=0, tiled=True
        ).astype(jnp.float32),
        lax.psum_scatter(
            grad_sums[3].astype(jnp.bfloat16), "ctx", scatter_dimension=1, tiled=True
        ).astype(jnp.float32),
        lax.psum_scatter(
            grad_sums[4].astype(jnp.bfloat16), "ctx", scatter_dimension=0, tiled=True
        ).astype(jnp.float32),
        lax.psum_scatter(
            grad_sums[5].astype(jnp.bfloat16), "ctx", scatter_dimension=0, tiled=True
        ).astype(jnp.float32),
        lax.psum_scatter(
            grad_sums[6].astype(jnp.bfloat16), "ctx", scatter_dimension=0, tiled=True
        ).astype(jnp.float32),
        lax.psum_scatter(
            grad_sums[7].astype(jnp.bfloat16), "ctx", scatter_dimension=1, tiled=True
        ).astype(jnp.float32),
    )
    return (section_out[None], input_grad[None]) + tuple((shard_now[None] for shard_now in reduced))


def swapped(value, axis, bit):
    count = lax.axis_size(axis)
    return lax.ppermute(value, axis, [(source, source ^ bit) for source in range(count)])


class Place:
    def __init__(self):
        self.section = lax.axis_index("section")
        self.ctx = lax.axis_index("ctx")
        tp = lax.axis_index("tp")
        self.low = tp % 2
        self.high = tp // 2
        self.ctx_count = lax.axis_size("ctx")


def gathered(rows):
    rows = jnp.concatenate(
        [rows] + [swapped(rows, "ctx", bit) for bit in range(1, lax.axis_size("ctx"))], axis=0
    )
    rows = jnp.concatenate([rows, swapped(rows, "tp", 2)], axis=0)
    return jnp.concatenate([rows, swapped(rows, "section", 1)], axis=0)


def scattered(rows):
    for axis, bit in (("section", 1), ("tp", 2)):
        half = rows.shape[0] // 2
        other = swapped(rows[half:].astype(jnp.bfloat16), axis, bit)
        rows = rows[:half].astype(jnp.float32) + other.astype(jnp.float32)
    count = lax.axis_size("ctx")
    blocks = rows.reshape(count, -1, rows.shape[1])
    total = blocks[0]
    for bit in range(1, count):
        total = total + swapped(blocks[bit].astype(jnp.bfloat16), "ctx", bit).astype(jnp.float32)
    return total


def relative_index(place, block):
    count = place.ctx_count
    ctx_at = jnp.arange(count, dtype=jnp.int32) ^ place.ctx
    high_at = jnp.arange(2, dtype=jnp.int32) ^ place.high
    section_at = jnp.arange(2, dtype=jnp.int32) ^ place.section
    index = (
        ctx_at[None, None, :, None] * (4 * block)
        + high_at[None, :, None, None] * (2 * block)
        + section_at[:, None, None, None] * block
        + jnp.arange(block, dtype=jnp.int32)[None, None, None, :]
    )
    return index.reshape(-1)


def section_pairs(layer, bit):
    count = lax.axis_size("ctx")
    return [(layer * count + source, layer * count + (source ^ bit)) for source in range(count)]


def home_pairs(layer, across):
    tp_count = lax.axis_size("tp")
    pairs = []
    for high in range(tp_count // 2):
        for low in range(2):
            source = layer * tp_count + high * 2 + low
            target = low * tp_count + high * 2 + (low ^ across)
            pairs.append((source, target))
    return pairs


def spread(pack, layer, place):
    count = place.ctx_count
    near, far = [], []
    for bit in range(count):
        block = lax.dynamic_index_in_dim(pack, place.ctx ^ bit, axis=0, keepdims=False)
        if bit:
            block = lax.ppermute(block, ("section", "ctx"), section_pairs(layer, bit))
        near.append(lax.ppermute(block, ("section", "tp"), home_pairs(layer, 0)))
        far.append(lax.ppermute(block, ("section", "tp"), home_pairs(layer, 1)))
    is_near = place.low == place.section
    used = jnp.stack([jnp.where(is_near, one, two) for one, two in zip(near, far)])
    used = jnp.concatenate(
        [
            lax.dynamic_index_in_dim(used, place.ctx ^ at, axis=0, keepdims=False)
            for at in range(count)
        ],
        axis=0,
    )
    return used


def collected(grad, layer, place):
    count = place.ctx_count
    grad = grad.astype(jnp.bfloat16)
    near = lax.ppermute(grad, ("section", "tp"), [(b, a) for a, b in home_pairs(layer, 0)])
    far = lax.ppermute(grad, ("section", "tp"), [(b, a) for a, b in home_pairs(layer, 1)])
    both = (near.astype(jnp.float32) + far.astype(jnp.float32)).astype(jnp.bfloat16)
    both = both.reshape(count, -1, both.shape[1])
    received = []
    for bit in range(count):
        block = lax.dynamic_index_in_dim(both, place.ctx ^ bit, axis=0, keepdims=False)
        if bit:
            block = lax.ppermute(block, ("section", "ctx"), section_pairs(layer, bit))
        received.append(block)
    received = jnp.stack(received)
    return [
        lax.dynamic_index_in_dim(received, place.ctx ^ at, axis=0, keepdims=False)
        for at in range(count)
    ]


def plane_rows(rows, place):
    block = rows.shape[0]
    rows = rows.astype(jnp.bfloat16)[None, None, None]
    rows = jnp.concatenate([rows, swapped(rows, "section", 1)], axis=2)
    rows = jnp.concatenate([rows, swapped(rows, "tp", 2)], axis=1)
    rows = jnp.concatenate([rows, swapped(rows, "tp", 1)], axis=0)
    for axis, at in ((0, place.low), (1, place.high), (2, place.section)):
        rows = jnp.where(at == 0, rows, jnp.flip(rows, axis))
    return rows.reshape(2, 4 * block, rows.shape[-1])


def attention_forward(query, key, value, causal, cosine, sine):
    heads = query.shape[1] // HEAD_WIDTH
    rows = query.shape[0]
    query = rotate(query.reshape(rows, heads, HEAD_WIDTH), cosine, sine).astype(jnp.bfloat16)
    key = rotate(key.reshape(rows, 1, HEAD_WIDTH), cosine, sine)[:, 0].astype(jnp.bfloat16)
    value = value.astype(jnp.bfloat16)
    scores = jnp.einsum("qhd,kd->hqk", query, key, preferred_element_type=jnp.float32) * 0.125
    scores = jnp.where(causal, scores, NEG)
    row_max = jnp.max(scores, axis=-1, keepdims=True)
    weights = jnp.exp(scores - row_max)
    row_total = jnp.sum(weights, axis=-1, keepdims=True)
    weighted = jnp.einsum(
        "hqk,kd->hqd", weights.astype(jnp.bfloat16), value, preferred_element_type=jnp.float32
    )
    attended = jnp.transpose(weighted / row_total, (1, 0, 2)).astype(jnp.bfloat16)
    return attended, (query, key, value, row_max + jnp.log(row_total))


def attention_backward(d_attended, attended, saved, causal, cosine, sine):
    query, key, value, log_total = saved
    rows, heads = query.shape[:2]
    d_attended = d_attended.astype(jnp.bfloat16).reshape(rows, heads, HEAD_WIDTH)
    delta = jnp.sum(d_attended.astype(jnp.float32) * attended.astype(jnp.float32), axis=-1)
    scores = jnp.einsum("qhd,kd->hqk", query, key, preferred_element_type=jnp.float32) * 0.125
    probs = jnp.where(causal, jnp.exp(scores - log_total), 0.0)
    d_prob = jnp.einsum("qhd,kd->hqk", d_attended, value, preferred_element_type=jnp.float32)
    d_score = (probs * (d_prob - delta.T[..., None]) * 0.125).astype(jnp.bfloat16)
    d_query = jnp.einsum("hqk,kd->qhd", d_score, key, preferred_element_type=jnp.float32)
    d_key = jnp.einsum("hqk,qhd->kd", d_score, query, preferred_element_type=jnp.float32)
    d_value = jnp.einsum(
        "hqk,qhd->kd", probs.astype(jnp.bfloat16), d_attended, preferred_element_type=jnp.float32
    )
    d_query = rotate(d_query, cosine, -sine).reshape(rows, -1)
    d_key = rotate(d_key[:, None], cosine, -sine)[:, 0]
    return jnp.concatenate([d_query, d_key, d_value], axis=-1).astype(jnp.bfloat16)


def dot_rows(left, right):
    return jnp.dot(left, right, preferred_element_type=jnp.float32)


def dot_back(left, right):
    return lax.dot_general(
        left, right, (((1,), (1,)), ((), ())), preferred_element_type=jnp.float32
    )


def dot_tokens(left, right):
    return lax.dot_general(
        left, right, (((0,), (0,)), ((), ())), preferred_element_type=jnp.float32
    )


def layer_ahead(rows, gains, attn_weights, ffn_weights, tables):
    causal, cosine, sine = tables
    gain_attn, gain_ffn = gains
    head_cols = attn_weights.shape[1] - 2 * HEAD_WIDTH
    head_cols = head_cols // 2
    hidden_cols = ffn_weights.shape[1] // 3
    rows_f = rows.astype(jnp.float32)
    normed1, inv1, attn_in = norm_forward(rows_f, gain_attn)
    attn_in = gathered(attn_in)
    qkv = dot_rows(attn_in, attn_weights[:, : head_cols + 2 * HEAD_WIDTH])
    attended, kept = attention_forward(
        qkv[:, :head_cols],
        qkv[:, head_cols : head_cols + HEAD_WIDTH],
        qkv[:, head_cols + HEAD_WIDTH :],
        causal,
        cosine,
        sine,
    )
    flat = attended.reshape(attended.shape[0], -1)
    hidden1 = rows_f + scattered(
        dot_back(flat, attn_weights[:, head_cols + 2 * HEAD_WIDTH :]).astype(jnp.bfloat16)
    )
    normed2, inv2, ffn_in = norm_forward(hidden1, gain_ffn)
    ffn_in = gathered(ffn_in)
    pre = dot_rows(ffn_in, ffn_weights[:, : 2 * hidden_cols])
    gate_pre, up_value = pre[:, :hidden_cols], pre[:, hidden_cols:]
    hidden = (jax.nn.silu(gate_pre) * up_value).astype(jnp.bfloat16)
    result = (
        hidden1
        + scattered(dot_back(hidden, ffn_weights[:, 2 * hidden_cols :]).astype(jnp.bfloat16))
    ).astype(jnp.bfloat16)
    saved = (
        (normed1, inv1, attn_in, attended, kept),
        (normed2, inv2, ffn_in, gate_pre, up_value, hidden),
    )
    return result, saved


def layer_back(upstream, gains, attn_weights, ffn_weights, tables, saved):
    causal, cosine, sine = tables
    gain_attn, gain_ffn = gains
    (normed1, inv1, attn_in, attended, kept), ffn_saved = saved
    normed2, inv2, ffn_in, gate_pre, up_value, hidden = ffn_saved
    head_cols = (attn_weights.shape[1] - 2 * HEAD_WIDTH) // 2
    hidden_cols = ffn_weights.shape[1] // 3
    above = gathered(upstream)
    d_hidden = dot_rows(above, ffn_weights[:, 2 * hidden_cols :])
    sigma = jax.nn.sigmoid(gate_pre)
    d_gate = d_hidden * up_value * sigma * (1.0 + gate_pre * (1.0 - sigma))
    d_up = d_hidden * gate_pre * sigma
    d_pre = jnp.concatenate([d_gate, d_up], axis=-1).astype(jnp.bfloat16)
    d_norm2 = scattered(dot_back(d_pre, ffn_weights[:, : 2 * hidden_cols]).astype(jnp.bfloat16))
    gain_grad2, d_resid = norm_backward(d_norm2, normed2, inv2, gain_ffn)
    d_hidden1 = upstream.astype(jnp.float32) + d_resid
    ffn_grad = jnp.concatenate(
        [
            dot_tokens(ffn_in, d_pre).astype(jnp.bfloat16),
            dot_tokens(above, hidden).astype(jnp.bfloat16),
        ],
        axis=-1,
    )
    d_rows = gathered(d_hidden1.astype(jnp.bfloat16))
    d_attended = dot_rows(d_rows, attn_weights[:, head_cols + 2 * HEAD_WIDTH :])
    d_qkv = attention_backward(d_attended, attended, kept, causal, cosine, sine)
    d_norm1 = scattered(
        dot_back(d_qkv, attn_weights[:, : head_cols + 2 * HEAD_WIDTH]).astype(jnp.bfloat16)
    )
    gain_grad1, d_front = norm_backward(d_norm1, normed1, inv1, gain_attn)
    attn_grad = jnp.concatenate(
        [
            dot_tokens(attn_in, d_qkv).astype(jnp.bfloat16),
            dot_tokens(d_rows, attended.reshape(attended.shape[0], -1)).astype(jnp.bfloat16),
        ],
        axis=-1,
    )
    d_input = (d_hidden1 + d_front).astype(jnp.bfloat16)
    return d_input, attn_grad, ffn_grad, gain_grad1, gain_grad2


def own_rows(array, place):
    block = array.shape[1] // 4
    start = (place.high * 2 + place.section) * block
    return lax.dynamic_slice(
        array, (place.low, start) + (0,) * (array.ndim - 2), (1, block) + array.shape[2:]
    )[0]


def whole_gain(gain, layer, place):
    count = place.ctx_count
    gain = gain.astype(jnp.bfloat16)
    other = swapped(gain, "section", 1)
    gain = jnp.where(place.section == layer, gain, other)
    blocks = jnp.stack([gain] + [swapped(gain, "ctx", bit) for bit in range(1, count)])
    return jnp.concatenate(
        [
            lax.dynamic_index_in_dim(blocks, place.ctx ^ at, axis=0, keepdims=False)
            for at in range(count)
        ],
        axis=-1,
    )


def on_device_relay(
    activations,
    positions,
    cotangent,
    attn_gain,
    w_query,
    w_keyval,
    w_out,
    ffn_gain,
    w_gate,
    w_up,
    w_down,
):
    place = Place()
    count = place.ctx_count
    layers = 2
    width = w_query.shape[1]
    head_cols = w_query.shape[2] // count
    hidden_cols = w_gate.shape[2] // count
    attn_pack = jnp.concatenate(
        [
            w_query[0].reshape(width, count, head_cols).transpose(1, 0, 2),
            jnp.broadcast_to(
                w_keyval[0].reshape(1, width, 2 * HEAD_WIDTH), (count, width, 2 * HEAD_WIDTH)
            ),
            w_out[0].reshape(count, head_cols, width).transpose(0, 2, 1),
        ],
        axis=-1,
    )
    ffn_pack = jnp.concatenate(
        [
            w_gate[0].reshape(width, count, hidden_cols).transpose(1, 0, 2),
            w_up[0].reshape(width, count, hidden_cols).transpose(1, 0, 2),
            w_down[0].reshape(count, hidden_cols, width).transpose(0, 2, 1),
        ],
        axis=-1,
    )
    gains_own = jnp.concatenate([attn_gain, ffn_gain], axis=0)
    block = activations.shape[1] // 4
    index = relative_index(place, block)
    causal = index[None, :] <= index[:, None]
    own_positions = jnp.broadcast_to(own_rows(positions, place)[:, None], (block, 128))
    cosine, sine = rope_tables(gathered(own_positions)[:, 0])
    tables = (causal, cosine, sine)
    rows = own_rows(activations, place)
    kept, outputs, used = [], [], []
    for layer in range(layers):
        both_gains = whole_gain(gains_own, layer, place)
        gains = (both_gains[0], both_gains[1])
        attn_weights = spread(attn_pack, layer, place)
        ffn_weights = spread(ffn_pack, layer, place)
        rows, saved = layer_ahead(rows, gains, attn_weights, ffn_weights, tables)
        used.append((gains, attn_weights, ffn_weights))
        kept.append(saved)
        outputs.append(plane_rows(rows, place))
    upstream = own_rows(cotangent, place)
    input_grads, gain_grads, attn_grads, ffn_grads = [None] * 2, [None] * 2, [None] * 2, [None] * 2
    for layer in reversed(range(layers)):
        gains, attn_weights, ffn_weights = used[layer]
        upstream, attn_grad, ffn_grad, gain1, gain2 = layer_back(
            upstream, gains, attn_weights, ffn_weights, tables, kept[layer]
        )
        ffn_grads[layer] = collected(ffn_grad, layer, place)
        attn_grads[layer] = collected(attn_grad, layer, place)
        gain_grads[layer] = (gain1, gain2)
        input_grads[layer] = plane_rows(upstream, place)
    front = place.section == 0

    def chosen(values):
        return jnp.where(front, values[0], values[1])

    section_out = chosen(outputs)
    input_grad = chosen(input_grads)
    gain_rows = jnp.stack([*gain_grads[0], *gain_grads[1]])
    gain_rows = gain_rows + swapped(gain_rows, "section", 1)
    gain_rows = gain_rows + swapped(gain_rows, "tp", 1)
    gain_rows = gain_rows + swapped(gain_rows, "tp", 2)
    gain_rows = gain_rows.reshape(2 * layers, count, width).transpose(1, 0, 2)
    total = lax.dynamic_index_in_dim(gain_rows, place.ctx, axis=0, keepdims=False)
    for bit in range(1, count):
        part = lax.dynamic_index_in_dim(gain_rows, place.ctx ^ bit, axis=0, keepdims=False)
        total = total + swapped(part, "ctx", bit)
    gain_total = jnp.where(front, total[:layers], total[layers:])
    ffn_blocks = [chosen(pair).astype(jnp.float32) for pair in zip(ffn_grads[0], ffn_grads[1])]
    attn_blocks = [chosen(pair).astype(jnp.float32) for pair in zip(attn_grads[0], attn_grads[1])]
    ends = head_cols + 2 * HEAD_WIDTH
    grad_query = jnp.concatenate([one[:, :head_cols] for one in attn_blocks], axis=-1)
    grad_keyval = sum(one[:, head_cols:ends] for one in attn_blocks)
    grad_out = jnp.concatenate([one[:, ends:].T for one in attn_blocks], axis=0)
    grad_gate = jnp.concatenate([one[:, :hidden_cols] for one in ffn_blocks], axis=-1)
    grad_up = jnp.concatenate([one[:, hidden_cols : 2 * hidden_cols] for one in ffn_blocks], axis=-1)
    grad_down = jnp.concatenate([one[:, 2 * hidden_cols :].T for one in ffn_blocks], axis=0)
    return (
        section_out[None],
        input_grad[None],
        gain_total[0][None],
        grad_query[None],
        grad_keyval.reshape(w_keyval.shape),
        grad_out[None],
        gain_total[1][None],
        grad_gate[None],
        grad_up[None],
        grad_down[None],
    )


def relay_fits(mesh):
    sizes = mesh.shape
    heads = 8
    return (
        sizes["section"] == 2
        and sizes["tp"] == 4
        and heads % sizes["ctx"] == 0
        and sizes["ctx"] & (sizes["ctx"] - 1) == 0
    )


def solution(mesh):
    placed = (
        P(None, "ctx", None),
        P(None, "ctx"),
        P(None, "ctx", None),
        P("section", "ctx"),
        P("section", "ctx", "tp"),
        P("section", "ctx", "tp", None),
        P("section", "tp", "ctx"),
        P("section", "ctx"),
        P("section", "ctx", "tp"),
        P("section", "ctx", "tp"),
        P("section", "tp", "ctx"),
    )
    return jax.shard_map(
        on_device_relay if relay_fits(mesh) else on_device,
        mesh=mesh,
        in_specs=placed,
        out_specs=(
            P("section", None, "ctx", None),
            P("section", None, "ctx", None),
            P("section", "ctx"),
            P("section", "ctx", "tp"),
            P("section", "ctx", "tp", None),
            P("section", "tp", "ctx"),
            P("section", "ctx"),
            P("section", "ctx", "tp"),
            P("section", "ctx", "tp"),
            P("section", "tp", "ctx"),
        ),
        check_vma=False,
    )
```

```python
import jax
import jax.numpy as jnp
from jax import lax
from jax.sharding import PartitionSpec as P

HEAD_WIDTH = 64


EPS = 1e-05
ROPE_BASE = 10000.0
NEG = -1e30


def passed_along(value, axis, steps):
    count = lax.axis_size(axis)
    initial, last = (max(0, -steps), min(count, count - steps))
    return lax.ppermute(value, axis, [(source, source + steps) for source in range(initial, last)])


def rope_tables(token_pos):
    half_dim = HEAD_WIDTH // 2
    frequency = ROPE_BASE ** (-(2.0 * jnp.arange(half_dim).astype(jnp.float32)) / HEAD_WIDTH)
    angles = token_pos.astype(jnp.float32)[:, None] * frequency[None, :]
    return (jnp.cos(angles)[:, None, :], jnp.sin(angles)[:, None, :])


def rotate(tensor, cosine, sine_part):
    front_half = tensor[..., : HEAD_WIDTH // 2]
    back_half = tensor[..., HEAD_WIDTH // 2 :]
    return jnp.concatenate(
        [front_half * cosine - back_half * sine_part, back_half * cosine + front_half * sine_part],
        axis=-1,
    )


def norm_forward(inputs_f, gain_row):
    mean_sq = jnp.mean(inputs_f * inputs_f, axis=-1, keepdims=True)
    inv_rms = lax.rsqrt(mean_sq + EPS)
    normed = inputs_f * inv_rms
    return (normed, inv_rms, (normed * gain_row.astype(jnp.float32)).astype(jnp.bfloat16))


def norm_backward(upstream_f, normed, inv_rms, gain_row):
    scaled = upstream_f * gain_row.astype(jnp.float32)
    gain_grad = jnp.sum(upstream_f * normed, axis=0)
    inner = jnp.mean(scaled * normed, axis=-1, keepdims=True)
    return (gain_grad, inv_rms * (scaled - normed * inner))


def head_sum(partial_now):
    return lax.psum(partial_now.astype(jnp.bfloat16), "tp").astype(jnp.float32)


def forward_layer(layer_in, token_pos, weights):
    (
        gain_attn,
        query_weight,
        key_value_weight,
        weight_out,
        gain_ffn,
        weight_gate,
        weight_up,
        weight_down,
    ) = weights
    token_rows = layer_in.shape[0]
    kv_local = key_value_weight.shape[1]
    heads_local = query_weight.shape[1] // HEAD_WIDTH
    query_group_width = heads_local // kv_local
    first_row = lax.axis_index("ctx") * token_rows
    inputs_f = layer_in.astype(jnp.float32)
    normed1, inv_rms1, first_normed_bfloat = norm_forward(inputs_f, gain_attn)
    cosine, sine_part = rope_tables(token_pos)
    query_proj = jnp.dot(
        first_normed_bfloat, query_weight, preferred_element_type=jnp.float32
    ).reshape(token_rows, heads_local, HEAD_WIDTH)
    key_value_projection = jnp.dot(
        first_normed_bfloat,
        key_value_weight.reshape(key_value_weight.shape[0], -1),
        preferred_element_type=jnp.float32,
    ).reshape(token_rows, kv_local, 2 * HEAD_WIDTH)
    query_rows = (
        rotate(query_proj, cosine, sine_part)
        .astype(jnp.bfloat16)
        .reshape(token_rows, kv_local, query_group_width, HEAD_WIDTH)
    )
    key_rows = rotate(key_value_projection[..., :HEAD_WIDTH], cosine, sine_part).astype(
        jnp.bfloat16
    )
    kv_block = jnp.concatenate(
        [key_rows, key_value_projection[..., HEAD_WIDTH:].astype(jnp.bfloat16)], axis=-1
    )
    query_index = first_row + jnp.arange(token_rows, dtype=jnp.int32)
    kv_piece = lax.all_gather(kv_block, "ctx", axis=0, tiled=True)
    row_max = jnp.full((kv_local, query_group_width, token_rows), NEG, jnp.float32)
    key_part = kv_piece[..., :HEAD_WIDTH]
    value_part = kv_piece[..., HEAD_WIDTH:]
    scores = (
        jnp.einsum("qhgd,khd->hgqk", query_rows, key_part, preferred_element_type=jnp.float32)
        * 0.125
    )
    key_index = jnp.arange(kv_piece.shape[0], dtype=jnp.int32)
    causal = key_index[None, :] <= query_index[:, None]
    scores = jnp.where(causal, scores, NEG)
    new_max = jnp.maximum(row_max, jnp.max(scores, axis=-1))
    weights_now = jnp.where(causal, jnp.exp(scores - new_max[..., None]), 0.0)
    row_total = jnp.sum(weights_now, axis=-1)
    weighted = jnp.einsum(
        "hgqk,khd->hgqd",
        weights_now.astype(jnp.bfloat16),
        value_part,
        preferred_element_type=jnp.float32,
    )
    row_max, row_total, weighted = (new_max, row_total, weighted)
    logarithm_total = row_max + jnp.log(row_total)
    attention_output = jnp.transpose(weighted / row_total[..., None], (2, 0, 1, 3)).astype(
        jnp.bfloat16
    )
    hidden1 = inputs_f + head_sum(
        jnp.dot(
            attention_output.reshape(token_rows, -1), weight_out, preferred_element_type=jnp.float32
        )
    )
    normed2, inv_rms2, normed_bf2 = norm_forward(hidden1, gain_ffn)
    gate_pre = jnp.dot(normed_bf2, weight_gate, preferred_element_type=jnp.float32)
    up_value = jnp.dot(normed_bf2, weight_up, preferred_element_type=jnp.float32)
    hidden = (jax.nn.silu(gate_pre) * up_value).astype(jnp.bfloat16)
    result = (
        hidden1 + head_sum(jnp.dot(hidden, weight_down, preferred_element_type=jnp.float32))
    ).astype(jnp.bfloat16)
    saved = (
        normed1,
        inv_rms1,
        first_normed_bfloat,
        query_rows,
        kv_block,
        attention_output,
        logarithm_total,
        normed2,
        inv_rms2,
        normed_bf2,
        gate_pre,
        up_value,
        hidden,
        cosine,
        sine_part,
    )
    return (result, saved)


def backward_layer(upstream, weights, saved):
    (
        gain_attn,
        query_weight,
        key_value_weight,
        weight_out,
        gain_ffn,
        weight_gate,
        weight_up,
        weight_down,
    ) = weights
    (
        normed1,
        inv_rms1,
        first_normed_bfloat,
        query_rows,
        kv_block,
        attention_output,
        logarithm_total,
        normed2,
        inv_rms2,
        normed_bf2,
        gate_pre,
        up_value,
        hidden,
        cosine,
        sine_part,
    ) = saved
    token_rows = upstream.shape[0]
    kv_local = kv_block.shape[1]
    query_group_width = query_rows.shape[2]
    first_row = lax.axis_index("ctx") * token_rows
    upstream_f = upstream.astype(jnp.float32)
    d_hidden = jnp.dot(upstream, weight_down.T, preferred_element_type=jnp.float32)
    grad_down = jnp.dot(hidden.T, upstream, preferred_element_type=jnp.float32)
    sigma = jax.nn.sigmoid(gate_pre)
    d_gate = (d_hidden * up_value * sigma * (1.0 + gate_pre * (1.0 - sigma))).astype(jnp.bfloat16)
    d_up = (d_hidden * gate_pre * sigma).astype(jnp.bfloat16)
    grad_gate = jnp.dot(normed_bf2.T, d_gate, preferred_element_type=jnp.float32)
    grad_up = jnp.dot(normed_bf2.T, d_up, preferred_element_type=jnp.float32)
    d_norm2 = head_sum(
        jnp.dot(d_gate, weight_gate.T, preferred_element_type=jnp.float32)
        + jnp.dot(d_up, weight_up.T, preferred_element_type=jnp.float32)
    )
    grad_gain2, d_resid = norm_backward(d_norm2, normed2, inv_rms2, gain_ffn)
    d_hidden1 = upstream_f + d_resid
    d_hidden_bf = d_hidden1.astype(jnp.bfloat16)
    grad_out = jnp.dot(
        attention_output.reshape(token_rows, -1).T, d_hidden_bf, preferred_element_type=jnp.float32
    )
    attention_output_gradient = jnp.dot(
        d_hidden_bf, weight_out.T, preferred_element_type=jnp.float32
    ).astype(jnp.bfloat16)
    attention_output_gradient = attention_output_gradient.reshape(
        token_rows, kv_local, query_group_width, HEAD_WIDTH
    )
    kv_whole = lax.all_gather(kv_block, "ctx", axis=0, tiled=True)
    total_rows = kv_whole.shape[0]
    key_rows_block = min(512, total_rows)
    block_count = total_rows // key_rows_block
    kv_blocks = kv_whole.reshape(block_count, key_rows_block, kv_local, 2 * HEAD_WIDTH)
    block_starts = jnp.arange(block_count, dtype=jnp.int32) * key_rows_block
    query_index = first_row + jnp.arange(token_rows, dtype=jnp.int32)
    delta_sum = jnp.transpose(
        jnp.sum(
            attention_output_gradient.astype(jnp.float32) * attention_output.astype(jnp.float32),
            axis=-1,
        ),
        (1, 2, 0),
    )

    def key_block(d_query_acc, packed):
        kv_piece, offset = packed
        key_part = kv_piece[..., :HEAD_WIDTH]
        value_part = kv_piece[..., HEAD_WIDTH:]
        key_index = offset + jnp.arange(key_rows_block, dtype=jnp.int32)
        causal = key_index[None, :] <= query_index[:, None]
        scores = (
            jnp.einsum("qhgd,khd->hgqk", query_rows, key_part, preferred_element_type=jnp.float32)
            * 0.125
        )
        scores = jnp.where(causal, scores, NEG)
        probs = jnp.where(causal, jnp.exp(scores - logarithm_total[..., None]), 0.0)
        probs_bf = probs.astype(jnp.bfloat16)
        d_prob = jnp.einsum(
            "qhgd,khd->hgqk",
            attention_output_gradient,
            value_part,
            preferred_element_type=jnp.float32,
        )
        d_score = (probs * (d_prob - delta_sum[..., None]) * 0.125).astype(jnp.bfloat16)
        d_query_acc = d_query_acc + jnp.einsum(
            "hgqk,khd->qhgd", d_score, key_part, preferred_element_type=jnp.float32
        )
        key_gradient = jnp.einsum(
            "hgqk,qhgd->khd", d_score, query_rows, preferred_element_type=jnp.float32
        )
        d_value = jnp.einsum(
            "hgqk,qhgd->khd",
            probs_bf,
            attention_output_gradient,
            preferred_element_type=jnp.float32,
        )
        return (d_query_acc, jnp.concatenate([key_gradient, d_value], axis=-1))

    query_start = jnp.zeros((token_rows, kv_local, query_group_width, HEAD_WIDTH), jnp.float32)
    d_query_raw, kv_terms = lax.scan(key_block, query_start, (kv_blocks, block_starts))
    kv_terms = kv_terms.reshape(total_rows, kv_local, 2 * HEAD_WIDTH)
    keyvalue_gradient = lax.psum_scatter(
        kv_terms.astype(jnp.bfloat16), "ctx", scatter_dimension=0, tiled=True
    ).astype(jnp.float32)
    query_gradient = (
        rotate(d_query_raw.reshape(token_rows, -1, HEAD_WIDTH), cosine, -sine_part)
        .astype(jnp.bfloat16)
        .reshape(token_rows, -1)
    )
    d_key_rot = rotate(keyvalue_gradient[..., :HEAD_WIDTH], cosine, -sine_part)
    key_value_gradient = (
        jnp.concatenate([d_key_rot, keyvalue_gradient[..., HEAD_WIDTH:]], axis=-1)
        .astype(jnp.bfloat16)
        .reshape(token_rows, -1)
    )
    grad_query = jnp.dot(first_normed_bfloat.T, query_gradient, preferred_element_type=jnp.float32)
    key_value_grads = jnp.dot(
        first_normed_bfloat.T, key_value_gradient, preferred_element_type=jnp.float32
    ).reshape(key_value_weight.shape)
    first_norm_gradient = head_sum(
        jnp.dot(query_gradient, query_weight.T, preferred_element_type=jnp.float32)
        + jnp.dot(
            key_value_gradient,
            key_value_weight.reshape(key_value_weight.shape[0], -1).T,
            preferred_element_type=jnp.float32,
        )
    )
    grad_gain1, d_front = norm_backward(first_norm_gradient, normed1, inv_rms1, gain_attn)
    d_input = (d_hidden1 + d_front).astype(jnp.bfloat16)
    return (
        d_input,
        (
            grad_gain1,
            grad_query,
            key_value_grads,
            grad_out,
            grad_gain2,
            grad_gate,
            grad_up,
            grad_down,
        ),
    )


def on_device(
    activations,
    positions,
    cotangent,
    attn_gain,
    w_query,
    w_keyval,
    w_out,
    ffn_gain,
    w_gate,
    w_up,
    w_down,
):
    front_section = lax.axis_index("section") == 0
    micro_count = activations.shape[0]
    local_parts = (
        attn_gain[0],
        w_query[0],
        w_keyval[0],
        w_out[0],
        ffn_gain[0],
        w_gate[0],
        w_up[0],
        w_down[0],
    )
    forward_weights = (
        lax.all_gather(local_parts[0], "ctx", axis=0, tiled=True),
        lax.all_gather(local_parts[1], "ctx", axis=0, tiled=True),
        lax.all_gather(local_parts[2], "ctx", axis=0, tiled=True),
        lax.all_gather(local_parts[3], "ctx", axis=1, tiled=True),
        lax.all_gather(local_parts[4], "ctx", axis=0, tiled=True),
        lax.all_gather(local_parts[5], "ctx", axis=0, tiled=True),
        lax.all_gather(local_parts[6], "ctx", axis=0, tiled=True),
        lax.all_gather(local_parts[7], "ctx", axis=1, tiled=True),
    )
    arrived = jnp.zeros_like(activations[0])
    results = []
    kept = []
    for moment in range(micro_count + 1):
        later = min(moment, micro_count - 1)
        earlier = max(moment - 1, 0)
        layer_in = jnp.where(front_section, activations[later], arrived)
        layer_pos = jnp.where(front_section, positions[later], positions[earlier])
        produced, saved = forward_layer(layer_in, layer_pos, forward_weights)
        results.append(produced)
        kept.append(saved)
        arrived = passed_along(produced, "section", 1)
    backward_weights = (
        lax.all_gather(local_parts[0], "ctx", axis=0, tiled=True),
        lax.all_gather(local_parts[1], "ctx", axis=0, tiled=True),
        lax.all_gather(local_parts[2], "ctx", axis=0, tiled=True),
        lax.all_gather(local_parts[3], "ctx", axis=1, tiled=True),
        lax.all_gather(local_parts[4], "ctx", axis=0, tiled=True),
        lax.all_gather(local_parts[5], "ctx", axis=0, tiled=True),
        lax.all_gather(local_parts[6], "ctx", axis=0, tiled=True),
        lax.all_gather(local_parts[7], "ctx", axis=1, tiled=True),
    )
    grad_sums = tuple((jnp.zeros(shard_now.shape, jnp.float32) for shard_now in backward_weights))
    reduced = tuple((jnp.zeros(shard_now.shape, jnp.float32) for shard_now in local_parts))
    returned = jnp.zeros_like(cotangent[0])
    sent = []
    for moment in range(micro_count + 1):
        later = min(moment, micro_count - 1)
        earlier = max(moment - 1, 0)
        upstream = jnp.where(front_section, returned, cotangent[later])
        saved = jax.tree.map(
            lambda front_val, back_val: jnp.where(front_section, front_val, back_val),
            kept[earlier],
            kept[later + 1],
        )
        live = jnp.where(front_section, moment >= 1, moment < micro_count)
        d_input, layer_grads = backward_layer(upstream, backward_weights, saved)
        grad_sums = tuple(
            (
                jnp.where(live, total_now + grad_now, total_now)
                for total_now, grad_now in zip(grad_sums, layer_grads)
            )
        )
        sent.append(d_input)
        returned = passed_along(d_input, "section", -1)
    section_out = jnp.stack(
        [
            jnp.where(front_section, results[micro_idx], results[micro_idx + 1])
            for micro_idx in range(micro_count)
        ]
    )
    input_grad = jnp.stack(
        [
            jnp.where(front_section, sent[micro_idx + 1], sent[micro_idx])
            for micro_idx in range(micro_count)
        ]
    )
    reduced = (
        lax.psum_scatter(
            grad_sums[0].astype(jnp.bfloat16), "ctx", scatter_dimension=0, tiled=True
        ).astype(jnp.float32),
        lax.psum_scatter(
            grad_sums[1].astype(jnp.bfloat16), "ctx", scatter_dimension=0, tiled=True
        ).astype(jnp.float32),
        lax.psum_scatter(
            grad_sums[2].astype(jnp.bfloat16), "ctx", scatter_dimension=0, tiled=True
        ).astype(jnp.float32),
        lax.psum_scatter(
            grad_sums[3].astype(jnp.bfloat16), "ctx", scatter_dimension=1, tiled=True
        ).astype(jnp.float32),
        lax.psum_scatter(
            grad_sums[4].astype(jnp.bfloat16), "ctx", scatter_dimension=0, tiled=True
        ).astype(jnp.float32),
        lax.psum_scatter(
            grad_sums[5].astype(jnp.bfloat16), "ctx", scatter_dimension=0, tiled=True
        ).astype(jnp.float32),
        lax.psum_scatter(
            grad_sums[6].astype(jnp.bfloat16), "ctx", scatter_dimension=0, tiled=True
        ).astype(jnp.float32),
        lax.psum_scatter(
            grad_sums[7].astype(jnp.bfloat16), "ctx", scatter_dimension=1, tiled=True
        ).astype(jnp.float32),
    )
    return (section_out[None], input_grad[None]) + tuple((shard_now[None] for shard_now in reduced))


def swapped(value, axis, bit):
    count = lax.axis_size(axis)
    return lax.ppermute(value, axis, [(source, source ^ bit) for source in range(count)])


def picked(blocks, at):
    return lax.dynamic_index_in_dim(blocks, at, axis=0, keepdims=False)


class Place:
    def __init__(self):
        self.section = lax.axis_index("section")
        self.ctx = lax.axis_index("ctx")
        tp = lax.axis_index("tp")
        self.low = tp % 2
        self.high = tp // 2
        self.ctx_count = lax.axis_size("ctx")
        self.front = self.section == 0


def gathered(rows):
    rows = jnp.concatenate(
        [rows] + [swapped(rows, "ctx", bit) for bit in range(1, lax.axis_size("ctx"))], axis=0
    )
    return jnp.concatenate([rows, swapped(rows, "section", 1)], axis=0)


def scattered(rows):
    half = rows.shape[0] // 2
    other = swapped(rows[half:], "section", 1)
    rows = rows[:half].astype(jnp.float32) + other.astype(jnp.float32)
    count = lax.axis_size("ctx")
    blocks = rows.reshape(count, -1, rows.shape[1])
    parts = [
        swapped(blocks[bit].astype(jnp.bfloat16), "ctx", bit) for bit in range(1, count)
    ]
    total = blocks[0]
    for part in parts:
        total = total + part.astype(jnp.float32)
    return total


def relative_index(place, block):
    ctx_at = jnp.arange(place.ctx_count, dtype=jnp.int32) ^ place.ctx
    section_at = jnp.arange(2, dtype=jnp.int32) ^ place.section
    index = (
        ctx_at[None, :, None] * (4 * block)
        + place.high * (2 * block)
        + section_at[:, None, None] * block
        + jnp.arange(block, dtype=jnp.int32)[None, None, :]
    )
    return index.reshape(-1)


def halves_swapped(pack, place):
    keep = picked(pack, place.section)
    other = swapped(picked(pack, 1 - place.section), "section", 1)
    return [jnp.where(place.front, keep, other), jnp.where(place.front, other, keep)]


def whole_width(pack, place):
    count = place.ctx_count
    blocks = []
    for bit in range(count):
        block = picked(pack, place.ctx ^ bit)
        blocks.append(swapped(block, "ctx", bit) if bit else block)
    blocks = jnp.stack(blocks)
    return jnp.concatenate([picked(blocks, place.ctx ^ at) for at in range(count)], axis=-1)


def all_groups(rows):
    half = rows.shape[1] // 2
    low = swapped(rows, "tp", 1)
    high = swapped(rows, "tp", 2)
    both = jnp.concatenate(
        [swapped(low[:, :half], "tp", 2), swapped(high[:, half:], "tp", 1)], axis=1
    )
    return [rows, low, high, both]


def group_sums(groups):
    own, low, high, both = groups
    half = own.shape[1] // 2
    from_high = swapped(both[:, :half], "tp", 2).astype(jnp.float32)
    from_low = swapped(both[:, half:], "tp", 1).astype(jnp.float32)
    low = jnp.concatenate(
        [(low[:, :half].astype(jnp.float32) + from_high).astype(jnp.bfloat16), low[:, half:]], axis=1
    )
    high = jnp.concatenate(
        [high[:, :half], (high[:, half:].astype(jnp.float32) + from_low).astype(jnp.bfloat16)], axis=1
    )
    low = swapped(low, "tp", 1).astype(jnp.float32)
    high = swapped(high, "tp", 2).astype(jnp.float32)
    return (own.astype(jnp.float32) + low + high).astype(jnp.bfloat16)


def own_width(rows, place):
    count = place.ctx_count
    width = rows.shape[1] // count
    blocks = []
    for bit in range(count):
        block = lax.dynamic_slice_in_dim(rows, (place.ctx ^ bit) * width, width, axis=1)
        blocks.append(swapped(block, "ctx", bit) if bit else block)
    blocks = jnp.stack(blocks)
    return jnp.stack([picked(blocks, place.ctx ^ at) for at in range(count)])


def plane_rows(rows, place):
    block = rows.shape[0]
    rows = rows.astype(jnp.bfloat16)[None, None, None]
    rows = jnp.concatenate([rows, swapped(rows, "section", 1)], axis=2)
    rows = jnp.concatenate([rows, swapped(rows, "tp", 2)], axis=1)
    rows = jnp.concatenate([rows, swapped(rows, "tp", 1)], axis=0)
    for axis, at in ((0, place.low), (1, place.high), (2, place.section)):
        rows = jnp.where(at == 0, rows, jnp.flip(rows, axis))
    return rows.reshape(2, 4 * block, rows.shape[-1])


def dot_rows(left, right):
    return jnp.dot(left, right, preferred_element_type=jnp.float32)


def dot_back(left, right):
    return lax.dot_general(
        left, right, (((1,), (1,)), ((), ())), preferred_element_type=jnp.float32
    )


def dot_tokens(left, right):
    return lax.dot_general(
        left, right, (((0,), (0,)), ((), ())), preferred_element_type=jnp.float32
    ).astype(jnp.bfloat16)


def groups_turned(columns):
    half = columns.shape[1] // 2
    return jnp.concatenate([columns[:, half:], columns[:, :half]], axis=1)


def rows_turned(rows):
    parts = rows.reshape(2, 2, -1, rows.shape[1])
    return jnp.flip(parts, axis=1).reshape(rows.shape)


def attention_forward(qkv, tables, place):
    causal, cosine, sine, cosine_own, sine_own = tables
    rows = qkv.shape[0]
    qkv = qkv.reshape(rows, -1, 2, HEAD_WIDTH)
    query = rotate(qkv[:, :, 0], cosine, sine).astype(jnp.bfloat16)
    own = rotate(qkv[:, :, 1], cosine_own, sine_own).astype(jnp.bfloat16).reshape(rows, -1)
    own = jnp.concatenate([own, swapped(groups_turned(own), "tp", 2)], axis=0)
    other = swapped(rows_turned(own), "section", 1)
    key = jnp.where(place.front, own, other).reshape(2 * rows, -1, HEAD_WIDTH)
    value = jnp.where(place.front, other, own).reshape(2 * rows, -1, HEAD_WIDTH)
    scores = jnp.einsum("qhd,khd->hqk", query, key, preferred_element_type=jnp.float32) * 0.125
    scores = jnp.where(causal, scores, NEG)
    row_max = jnp.max(scores, axis=-1, keepdims=True)
    weights = jnp.exp(scores - row_max)
    row_total = jnp.sum(weights, axis=-1, keepdims=True)
    weighted = jnp.einsum(
        "hqk,khd->hqd", weights.astype(jnp.bfloat16), value, preferred_element_type=jnp.float32
    )
    attended = jnp.transpose(weighted / row_total, (1, 0, 2)).astype(jnp.bfloat16)
    return attended, (query, key, value, row_max + jnp.log(row_total))


def attention_backward(d_attended, attended, saved, tables, place):
    causal, cosine, sine, cosine_own, sine_own = tables
    query, key, value, log_total = saved
    rows, heads = query.shape[:2]
    d_attended = d_attended.astype(jnp.bfloat16).reshape(rows, heads, HEAD_WIDTH)
    delta = jnp.sum(d_attended.astype(jnp.float32) * attended.astype(jnp.float32), axis=-1)
    scores = jnp.einsum("qhd,khd->hqk", query, key, preferred_element_type=jnp.float32) * 0.125
    probs = jnp.where(causal, jnp.exp(scores - log_total), 0.0)
    d_prob = jnp.einsum("qhd,khd->hqk", d_attended, value, preferred_element_type=jnp.float32)
    d_score = (probs * (d_prob - delta.T[..., None]) * 0.125).astype(jnp.bfloat16)
    d_query = jnp.einsum("hqk,khd->qhd", d_score, key, preferred_element_type=jnp.float32)
    d_key = jnp.einsum("hqk,qhd->khd", d_score, query, preferred_element_type=jnp.float32)
    d_value = jnp.einsum(
        "hqk,qhd->khd", probs.astype(jnp.bfloat16), d_attended, preferred_element_type=jnp.float32
    )
    d_key = d_key.astype(jnp.bfloat16).reshape(2 * rows, -1)
    d_value = d_value.astype(jnp.bfloat16).reshape(2 * rows, -1)
    other = swapped(rows_turned(jnp.where(place.front, d_value, d_key)), "section", 1)
    own = jnp.where(place.front, d_key, d_value).astype(jnp.float32) + other.astype(jnp.float32)
    turned = groups_turned(own[rows:].astype(jnp.bfloat16))
    own = own[:rows] + swapped(turned, "tp", 2).astype(jnp.float32)
    own = rotate(own.reshape(rows, heads, HEAD_WIDTH), cosine_own, -sine_own)
    d_query = rotate(d_query, cosine, -sine)
    return jnp.stack([d_query, own], axis=2).astype(jnp.bfloat16).reshape(rows, -1)


def layer_ahead(rows_f, normed, gains, attn_weights, ffn_weights, tables, place):
    normed1, inv1, attn_in = normed
    w_qkv, w_back = attn_weights
    w_gate, w_up, w_down = ffn_weights
    qkv = dot_back(attn_in, w_qkv)
    attended, kept = attention_forward(qkv, tables, place)
    flat = attended.reshape(attended.shape[0], -1)
    hidden1 = rows_f + scattered(dot_rows(flat, w_back).astype(jnp.bfloat16))
    normed2, inv2, ffn_in = norm_forward(hidden1, gains[1])
    ffn_in = gathered(ffn_in)
    gate_pre = dot_back(ffn_in, w_gate)
    up_value = dot_back(ffn_in, w_up)
    hidden = (jax.nn.silu(gate_pre) * up_value).astype(jnp.bfloat16)
    result = (hidden1 + scattered(dot_rows(hidden, w_down).astype(jnp.bfloat16))).astype(
        jnp.bfloat16
    )
    saved = (
        (normed1, inv1, attn_in, attended, kept),
        (normed2, inv2, ffn_in, gate_pre, up_value, hidden),
    )
    return result, saved


def layer_back(upstream, gains, attn_weights, ffn_weights, tables, saved, place):
    w_qkv, w_back = attn_weights
    w_gate, w_up, w_down = ffn_weights
    (normed1, inv1, attn_in, attended, kept), ffn_saved = saved
    normed2, inv2, ffn_in, gate_pre, up_value, hidden = ffn_saved
    above = gathered(upstream)
    d_hidden = dot_back(above, w_down)
    sigma = jax.nn.sigmoid(gate_pre)
    d_gate = (d_hidden * up_value * sigma * (1.0 + gate_pre * (1.0 - sigma))).astype(jnp.bfloat16)
    d_up = (d_hidden * gate_pre * sigma).astype(jnp.bfloat16)
    d_norm2 = scattered((dot_rows(d_gate, w_gate) + dot_rows(d_up, w_up)).astype(jnp.bfloat16))
    ffn_grads = (dot_tokens(d_gate, ffn_in), dot_tokens(d_up, ffn_in), dot_tokens(hidden, above))
    gain_grad2, d_resid = norm_backward(d_norm2, normed2, inv2, gains[1])
    d_hidden1 = upstream.astype(jnp.float32) + d_resid
    d_rows = gathered(d_hidden1.astype(jnp.bfloat16))
    d_attended = dot_back(d_rows, w_back)
    d_qkv = attention_backward(d_attended, attended, kept, tables, place)
    d_norm1 = scattered(dot_rows(d_qkv, w_qkv).astype(jnp.bfloat16))
    flat = attended.reshape(attended.shape[0], -1)
    attn_grads = (dot_tokens(d_qkv, attn_in), dot_tokens(flat, d_rows))
    gain_grad1, d_front = norm_backward(d_norm1, normed1, inv1, gains[0])
    d_input = (d_hidden1 + d_front).astype(jnp.bfloat16)
    return d_input, attn_grads, ffn_grads, gain_grad1, gain_grad2


def own_rows(array, place):
    block = array.shape[1] // 4
    start = (place.high * 2 + place.section) * block
    return lax.dynamic_slice(
        array, (place.low, start) + (0,) * (array.ndim - 2), (1, block) + array.shape[2:]
    )[0]


def group_rows(groups, sizes):
    parts, start = [], 0
    for size in sizes:
        parts.append(jnp.concatenate([one[start : start + size] for one in groups], axis=0))
        start += size
    return parts


def group_packs(parts, sizes):
    return [
        jnp.concatenate(
            [part[at * size : (at + 1) * size] for part, size in zip(parts, sizes)], axis=0
        )
        for at in range(4)
    ]


def on_device_relay(
    activations,
    positions,
    cotangent,
    attn_gain,
    w_query,
    w_keyval,
    w_out,
    ffn_gain,
    w_gate,
    w_up,
    w_down,
):
    place = Place()
    count = place.ctx_count
    width = w_query.shape[1]
    whole = width * count
    head_rows = w_query.shape[2] // (2 * count)
    unit_rows = w_gate.shape[2] // (2 * count)
    pad = 8
    rows = own_rows(activations, place)
    block = rows.shape[0]

    def parted(array, size):
        return array.reshape(count, 2, size, width).transpose(1, 0, 2, 3)

    key_value = w_keyval.reshape(width, 2, HEAD_WIDTH).transpose(1, 2, 0)
    gain_rows = jnp.concatenate(
        [attn_gain, ffn_gain, jnp.zeros((pad - 2, width), jnp.bfloat16)], axis=0
    )
    attn_pack = jnp.concatenate(
        [
            parted(w_query[0].T, head_rows),
            jnp.broadcast_to(key_value[:, None], (2, count, HEAD_WIDTH, width)),
            parted(w_out[0], head_rows),
            jnp.broadcast_to(gain_rows, (2, count, pad, width)),
        ],
        axis=2,
    )
    ffn_pack = jnp.concatenate(
        [
            parted(w_gate[0].T, unit_rows),
            parted(w_up[0].T, unit_rows),
            parted(w_down[0], unit_rows),
        ],
        axis=2,
    )
    attn_sizes = (head_rows + HEAD_WIDTH, head_rows)
    ffn_sizes = (unit_rows,) * 3
    attn_halves = halves_swapped(attn_pack, place)
    ffn_halves = halves_swapped(ffn_pack, place)

    index = relative_index(place, block)
    partner = index + (1 - 2 * place.high) * (2 * block)
    causal = jnp.concatenate([index, partner])[None, :] <= index[:, None]
    token_pos = own_rows(positions, place)
    extra = jnp.stack([token_pos // 16, token_pos % 16], axis=-1).astype(jnp.bfloat16)
    extra = jnp.concatenate([extra, jnp.zeros((block, 126), jnp.bfloat16)], axis=-1)
    first = gathered(jnp.concatenate([rows, extra], axis=-1))
    token_pos = first[:, whole].astype(jnp.float32) * 16.0 + first[:, whole + 1].astype(jnp.float32)
    cosine, sine = rope_tables(token_pos)
    tables = (
        causal,
        cosine,
        sine,
        jnp.where(place.front, cosine, 1.0),
        jnp.where(place.front, sine, 0.0),
    )

    kept, outputs, used = [], [], []
    for layer in range(2):
        attn_pack = whole_width(attn_halves[layer], place)
        gains = (attn_pack[-pad], attn_pack[1 - pad])
        attn_weights = group_rows(all_groups(attn_pack[:-pad]), attn_sizes)
        ffn_weights = group_rows(
            all_groups(whole_width(ffn_halves[layer], place)), ffn_sizes
        )
        rows_f = rows.astype(jnp.float32)
        normed1, inv1, attn_in = norm_forward(rows_f, gains[0])
        if layer == 0:
            attn_in = norm_forward(first[:, :whole].astype(jnp.float32), gains[0])[2]
        else:
            attn_in = gathered(attn_in)
        rows, saved = layer_ahead(
            rows_f, (normed1, inv1, attn_in), gains, attn_weights, ffn_weights, tables, place
        )
        used.append((gains, attn_weights, ffn_weights))
        kept.append(saved)
        outputs.append(plane_rows(rows, place))

    upstream = own_rows(cotangent, place)
    input_grads, gain_grads, attn_grads, ffn_grads = [None] * 2, [None] * 2, [None] * 2, [None] * 2
    for layer in (1, 0):
        gains, attn_weights, ffn_weights = used[layer]
        upstream, attn_parts, ffn_parts, gain1, gain2 = layer_back(
            upstream, gains, attn_weights, ffn_weights, tables, kept[layer], place
        )
        home = [(1 - layer, layer)]
        for parts, sizes, grads in (
            (ffn_parts, ffn_sizes, ffn_grads),
            (attn_parts, attn_sizes, attn_grads),
        ):
            mine = own_width(group_sums(group_packs(parts, sizes)), place)
            grads[layer] = (mine, lax.ppermute(mine, "section", home))
        gain_grads[layer] = (gain1, gain2)
        input_grads[layer] = plane_rows(upstream, place)

    def chosen(values):
        return jnp.where(place.front, values[0], values[1])

    def joined(grads):
        mine = chosen([grads[0][0], grads[1][0]])
        other = chosen([grads[0][1], grads[1][1]])
        return jnp.stack(
            [jnp.where(place.front, mine, other), jnp.where(place.front, other, mine)], axis=1
        )

    section_out = chosen(outputs)
    input_grad = chosen(input_grads)
    gain_sums = jnp.stack([*gain_grads[0], *gain_grads[1]])
    gain_sums = gain_sums + swapped(gain_sums, "section", 1)
    gain_sums = gain_sums + swapped(gain_sums, "tp", 1)
    gain_sums = gain_sums + swapped(gain_sums, "tp", 2)
    gain_sums = gain_sums.reshape(4, count, width).transpose(1, 0, 2)
    total = picked(gain_sums, place.ctx)
    for bit in range(1, count):
        total = total + swapped(picked(gain_sums, place.ctx ^ bit), "ctx", bit)
    gain_total = jnp.where(place.front, total[:2], total[2:])
    ffn_all = joined(ffn_grads).astype(jnp.float32)
    attn_all = joined(attn_grads).astype(jnp.float32)

    def unparted(array, start, size):
        return array[:, :, start : start + size].reshape(-1, width)

    key_value = jnp.sum(attn_all[:, :, head_rows : head_rows + HEAD_WIDTH], axis=0)
    return (
        section_out[None],
        input_grad[None],
        gain_total[0][None],
        unparted(attn_all, 0, head_rows).T[None],
        key_value.transpose(2, 0, 1).reshape(w_keyval.shape),
        unparted(attn_all, head_rows + HEAD_WIDTH, head_rows)[None],
        gain_total[1][None],
        unparted(ffn_all, 0, unit_rows).T[None],
        unparted(ffn_all, unit_rows, unit_rows).T[None],
        unparted(ffn_all, 2 * unit_rows, unit_rows)[None],
    )


def relay_fits(mesh):
    sizes = mesh.shape
    return sizes["section"] == 2 and sizes["tp"] == 4 and sizes["ctx"] == 4


def solution(mesh):
    placed = (
        P(None, "ctx", None),
        P(None, "ctx"),
        P(None, "ctx", None),
        P("section", "ctx"),
        P("section", "ctx", "tp"),
        P("section", "ctx", "tp", None),
        P("section", "tp", "ctx"),
        P("section", "ctx"),
        P("section", "ctx", "tp"),
        P("section", "ctx", "tp"),
        P("section", "tp", "ctx"),
    )
    return jax.shard_map(
        on_device_relay if relay_fits(mesh) else on_device,
        mesh=mesh,
        in_specs=placed,
        out_specs=(
            P("section", None, "ctx", None),
            P("section", None, "ctx", None),
            P("section", "ctx"),
            P("section", "ctx", "tp"),
            P("section", "ctx", "tp", None),
            P("section", "tp", "ctx"),
            P("section", "ctx"),
            P("section", "ctx", "tp"),
            P("section", "ctx", "tp"),
            P("section", "tp", "ctx"),
        ),
        check_vma=False,
    )
```
